32 devices in a mesh: groups: 2 (over y), pb: 16 (over z, x, core).
Axes of the slice: x: 2, y: 2, z: 4, core: 2. Of those that a mesh axis runs over, the one named last changes fastest.
Arguments:
- fields: float32 [32, 16, 512], P(('groups', 'pb')), parts along dimension 0, may hold values from -6 to 6
- field_shift: float32 [16, 512], replicated, may hold values from -1 to 1
- cholesky: bfloat16 [512, 1024, 1024], P(None, 'pb'), may hold values from -0.015625 to 0.015625
- onebody: float32 [16, 64], replicated, may hold values from -0.5 to 0.5
- walkers: bfloat16 [32, 1024, 256], P(('groups', 'pb')), parts along dimension 0, may hold values from -6 to 6
Outputs:
- propagated: bfloat16 [32, 1024, 256], P(('groups', 'pb')), parts along dimension 0
The draws below stay inside these ranges and needn't reach their ends.
There are 2 independent parts, one for each index of `groups`. The reference program is written for one: setup_inputs(seed, part) draws one part's arguments, and reference() takes and returns one part's arrays. A program takes and returns all parts, laid end to end along the dimension named above; an argument that names none is the same for every part. Nothing has to cross between parts.
All inputs are finite; a program needn't handle non-finite values.
Results may differ from the reference program's by a relative error of at most 0.0089.
Values may be sent and summed in bfloat16 or wider, within the bound.
A program may use at most 192 MiB of HBM per device.

```python
import jax
import jax.numpy as jnp
from jax import lax

NK = 16
NORB = 64
NCHOL = 512
COLS = 256
TERMS = 6
WALKERS = 16


def level_of(key, shape, shards, smallest, largest):
    factor_of = 1.0
    for position, shards_of in shards:
        steps = jax.random.uniform(jax.random.fold_in(jax.random.fold_in(key, 6), position), (shards_of,), jnp.float32, smallest / len(shards), largest / len(shards))
        factor_of = factor_of * jnp.repeat(jnp.exp(steps), shape[position] // shards_of).reshape((-1,) + (1,) * (len(shape) - 1 - position))
    return factor_of


def gaussian(stream_key, extent, width, bound, shards=(), dtype=jnp.bfloat16):
    level = level_of(stream_key, extent, shards, -0.22, 0.18) if shards else 1.0
    entries = jax.random.normal(stream_key, extent, jnp.float32) * width * level
    return jnp.minimum(jnp.maximum(entries, -bound), bound).astype(dtype)


def setup_inputs(seed: int = 0, part: int = 0) -> dict:
    keys = jax.random.split(jax.random.key(seed), 6)
    part_splits = jax.random.split(jax.random.fold_in(keys[5], part), 6)
    return {
        "fields": gaussian(part_splits[0], (WALKERS, NK, NCHOL), 1.0, 6.0, ((0, 16),), jnp.float32),
        "field_shift": jnp.clip(jax.random.uniform(keys[1], (NK, NCHOL), jnp.float32, -1.0, 1.0), -1.0, 1.0),
        "cholesky": gaussian(keys[2], (NCHOL, NK * NORB, NK * NORB), (NCHOL * NK * NORB // 4) ** -0.5, 0.015625, ((1, 16),)),
        "onebody": jnp.clip(jax.random.uniform(keys[3], (NK, NORB), jnp.float32, -0.5, 0.5), -0.5, 0.5),
        "walkers": gaussian(part_splits[4], (WALKERS, NK * NORB, COLS), 1.0, 6.0, ((0, 16),)),
    }


def taylor(potential, determinant, onebody):
    term = determinant
    total = determinant.astype(jnp.float32)
    for order in range(1, TERMS):
        rolled = jnp.stack([jnp.roll(term, transfer, axis=0) for transfer in range(NK)], axis=1)
        rolled = rolled.reshape(NK, NK * NORB, COLS)
        product = jnp.einsum("kaj,kjc->kac", potential.astype(jnp.float32), rolled.astype(jnp.float32), precision=lax.Precision.HIGHEST)
        product = product + onebody[:, :, None] * term.astype(jnp.float32)
        term = (product * (-1.0 / order)).astype(jnp.bfloat16)
        total = total + term.astype(jnp.float32)
    return total.astype(jnp.bfloat16)


def reference(fields, field_shift, cholesky, onebody, walkers):
    count = fields.shape[0]
    shifted = (fields + field_shift[None]).astype(jnp.bfloat16)
    blocks = []
    for transfer in range(NK):
        slab = cholesky[:, transfer * NORB:(transfer + 1) * NORB, :].reshape(NCHOL, NORB * NK * NORB)
        blocks.append(jnp.dot(shifted[:, transfer, :], slab, preferred_element_type=jnp.float32).astype(jnp.bfloat16))
    potential_all = jnp.stack(blocks, axis=1).reshape(count, NK, NORB, NK, NORB)

    def propagate(pair):
        blocks_one, determinant = pair
        potential = blocks_one.transpose(2, 1, 0, 3).reshape(NK, NORB, NK * NORB)
        result = taylor(potential, determinant.reshape(NK, NORB, COLS), onebody)
        return result.reshape(NK * NORB, COLS)

    return lax.map(propagate, (potential_all, walkers))
```

```python
import functools

import jax
import jax.numpy as jnp
import numpy as np
from jax import lax
from jax.experimental import pallas as pl
from jax.experimental.pallas import tpu as pltpu
from jax.sharding import PartitionSpec as P

TERMS = 6
MESH = pl.DeviceIdType.MESH
ROWS = 16
SLOTS = 3
SPLITS = 2
PIECE = 2048


def plain(fields, field_shift, cholesky, onebody, walkers):
    devices = lax.axis_size("pb")
    local_walkers = fields.shape[0]
    kpoints = field_shift.shape[0]
    orbitals = onebody.shape[1]
    vectors = field_shift.shape[1]
    rows_here = cholesky.shape[1]
    per_transfer = orbitals // rows_here
    slab = cholesky.reshape(vectors, rows_here * kpoints * orbitals)
    shifted = (fields + field_shift[None]).astype(jnp.bfloat16)
    outgoing = jnp.repeat(shifted, per_transfer, axis=1)
    arrived = lax.all_to_all(outgoing, "pb", split_axis=1, concat_axis=0, tiled=True)
    partial_blocks = jnp.dot(arrived[:, 0, :], slab, preferred_element_type=jnp.float32).astype(
        jnp.bfloat16
    )
    outgoing_blocks = partial_blocks.reshape(devices, local_walkers, rows_here * kpoints * orbitals)
    relayed = lax.all_to_all(outgoing_blocks, "pb", split_axis=0, concat_axis=0, tiled=True)
    relayed = relayed.reshape(kpoints, per_transfer, local_walkers, rows_here, kpoints, orbitals)
    potential = relayed.transpose(2, 4, 1, 3, 0, 5).reshape(
        local_walkers, kpoints, orbitals, kpoints, orbitals
    )
    source_table = (np.arange(kpoints)[:, None] - np.arange(kpoints)[None, :]) % kpoints
    source_index = jnp.asarray(source_table.reshape(1, kpoints, 1, kpoints, 1), dtype=jnp.int32)
    permuted = jnp.take_along_axis(potential, source_index, axis=3)
    permuted = permuted.reshape(local_walkers, kpoints * orbitals, kpoints * orbitals)
    diagonal_term = onebody.reshape(kpoints * orbitals)[None, :, None]
    term = walkers
    total = term.astype(jnp.float32)
    for order in range(1, TERMS):
        product = jnp.einsum("wij,wjc->wic", permuted, term, preferred_element_type=jnp.float32)
        product = product + diagonal_term * term.astype(jnp.float32)
        term = (product * (-1.0 / order)).astype(jnp.bfloat16)
        total = total + term.astype(jnp.float32)
    return total.astype(jnp.bfloat16)


def kernel(
    n, nk, norb, fields_ref, shift_ref, chol_ref, onebody_ref, walker_ref, out_ref,
    fields_in, spread, left, buf, acc, blocks_out, blocks_in, matrix, diag, total, term_a, term_b,
    fsend, frecv, csem, bsend, brecv,
):
    me = lax.axis_index("pb")
    nchol = chol_ref.shape[0]
    cols = chol_ref.shape[2] // SPLITS
    row_blocks = norb // ROWS
    chunks = row_blocks * SPLITS
    k_here = cols // norb
    order = sorted(range(1, n), key=lambda d: abs(2 * d - n))
    group = 128
    wide = group * ROWS

    def tensor_copy(c, slot):
        i, h = c // SPLITS, c % SPLITS
        return pltpu.make_async_copy(
            chol_ref.at[:, pl.ds(pl.multiple_of(i * ROWS, ROWS), ROWS), pl.ds(pl.multiple_of(h * cols, cols), cols)],
            buf.at[slot],
            csem.at[slot],
        )

    for c in range(min(SLOTS, chunks)):
        tensor_copy(c, c).start()

    barrier = pltpu.get_barrier_semaphore()
    for d in order:
        pl.semaphore_signal(barrier, inc=1, device_id={"pb": lax.rem(me + d, n)}, device_id_type=MESH)
    pl.semaphore_wait(barrier, n - 1)

    def field_copy(peer, slot, k):
        return pltpu.make_async_remote_copy(
            src_ref=fields_ref.at[peer], dst_ref=fields_in.at[slot], send_sem=fsend.at[k],
            recv_sem=frecv.at[slot], device_id={"pb": peer}, device_id_type=MESH,
        )

    for k, d in enumerate(order):
        field_copy(lax.rem(me + d, n), me, k).start()
    fields_in[me] = fields_ref[me]

    spread[...] = (
        lax.broadcasted_iota(jnp.int32, (group, wide), 1) // ROWS
        == lax.broadcasted_iota(jnp.int32, (group, wide), 0)
    ).astype(jnp.float32).astype(jnp.bfloat16)
    square = lax.broadcasted_iota(jnp.int32, (norb, norb), 0) == lax.broadcasted_iota(
        jnp.int32, (norb, norb), 1
    )
    for k in range(nk):
        row = jnp.broadcast_to(onebody_ref[k : k + 1, :], (norb, norb))
        column = jnp.sum(jnp.where(square, row, 0.0), axis=1, keepdims=True)
        diag[k * norb : (k + 1) * norb, :] = jnp.broadcast_to(column, (norb, 128))

    for k, d in enumerate(order):
        peer = lax.rem(me + n - d, n)
        field_copy(peer, peer, k).wait_recv()

    shifted = (fields_in[:, 0, :] + shift_ref[pl.ds(me, 1), :]).astype(jnp.bfloat16)
    mask = (
        lax.broadcasted_iota(jnp.int32, (ROWS, wide), 1) % ROWS
        == lax.broadcasted_iota(jnp.int32, (ROWS, wide), 0)
    )
    for b in range(nchol // group):
        spreaded = jnp.dot(
            shifted[:, b * group : (b + 1) * group], spread[...], preferred_element_type=jnp.float32
        )
        for w in range(n):
            line = jnp.broadcast_to(spreaded[w : w + 1, :], (ROWS, wide))
            left[w * ROWS : (w + 1) * ROWS, b * wide : (b + 1) * wide] = jnp.where(
                mask, line, 0.0
            ).astype(jnp.bfloat16)

    def block_copy(c, peer, slot, k):
        return pltpu.make_async_remote_copy(
            src_ref=blocks_out.at[c, peer], dst_ref=blocks_in.at[c, slot], send_sem=bsend.at[c, k],
            recv_sem=brecv.at[c, slot], device_id={"pb": peer}, device_id_type=MESH,
        )

    vectors_piece = PIECE // ROWS

    def compute(c, carry):
        slot = lax.rem(c, SLOTS)
        tensor_copy(c, slot).wait()

        def piece(p, carry):
            right = buf[slot, pl.ds(p * vectors_piece, vectors_piece)].reshape(PIECE, cols)
            part = jnp.dot(
                left[:, pl.ds(pl.multiple_of(p * PIECE, PIECE), PIECE)], right,
                preferred_element_type=jnp.float32,
            )

            @pl.when(p == 0)
            def _():
                acc[...] = part

            @pl.when(p > 0)
            def _():
                acc[...] += part

            return carry

        lax.fori_loop(0, nchol // vectors_piece, piece, 0)

        @pl.when(c + SLOTS < chunks)
        def _():
            tensor_copy(c + SLOTS, slot).start()

        blocks_out[c] = acc[...].astype(jnp.bfloat16).reshape(n, ROWS, cols)
        for k, d in enumerate(order):
            block_copy(c, lax.rem(me + d, n), me, k).start()
        blocks_in[c, me] = blocks_out[c, me]
        return carry

    lax.fori_loop(0, chunks, compute, 0)

    def assemble(c, carry):
        i, h = c // SPLITS, c % SPLITS
        for k, d in enumerate(order):
            peer = lax.rem(me + n - d, n)
            block_copy(c, peer, peer, k).wait_recv()
        for kk in range(k_here):
            k = h * k_here + kk
            lane = kk // 2 * 128
            half = kk % 2 * norb
            rows = pl.ds(pl.multiple_of(k * norb + i * ROWS, ROWS), ROWS)
            for pair in range(nk // 2):
                first = blocks_in[c, lax.rem(k - 2 * pair + nk, nk), :, lane : lane + 128]
                second = blocks_in[c, lax.rem(k - 2 * pair - 1 + nk, nk), :, lane : lane + 128]
                matrix[rows, pair * 128 : (pair + 1) * 128] = jnp.concatenate(
                    [first[:, half : half + norb], second[:, half : half + norb]], axis=1
                )
        return carry

    lax.fori_loop(0, chunks, assemble, 0)

    size = nk * norb
    step = 256
    for number in range(1, TERMS):
        source = walker_ref if number == 1 else (term_a if number % 2 == 0 else term_b)
        target = term_a if number % 2 == 1 else term_b
        for r in range(0, size, step):
            rows = slice(r, r + step)
            product = jnp.dot(matrix[rows, :], source[...], preferred_element_type=jnp.float32)
            here = source[rows, :].astype(jnp.float32)
            weight = diag[rows, :]
            weight = jnp.concatenate([weight] * (here.shape[1] // 128), axis=1)
            product = product + weight * here
            term = (product * (-1.0 / number)).astype(jnp.bfloat16)
            before = here if number == 1 else total[rows, :]
            after = before + term.astype(jnp.float32)
            if number < TERMS - 1:
                target[rows, :] = term
                total[rows, :] = after
            else:
                out_ref[rows, :] = after.astype(jnp.bfloat16)

    for k, d in enumerate(order):
        field_copy(lax.rem(me + d, n), me, k).wait_send()

    def drain(c, carry):
        for k, d in enumerate(order):
            block_copy(c, lax.rem(me + d, n), me, k).wait_send()
        return carry

    lax.fori_loop(0, chunks, drain, 0)


def fused(fields, field_shift, cholesky, onebody, walkers):
    n = lax.axis_size("pb")
    nk, norb = onebody.shape
    nchol = cholesky.shape[0]
    width = cholesky.shape[2]
    cols = width // SPLITS
    chunks = norb // ROWS * SPLITS
    size, columns = walkers.shape[1:]
    bf16, f32 = jnp.bfloat16, jnp.float32
    vmem = pl.BlockSpec(memory_space=pltpu.VMEM)
    out = pl.pallas_call(
        functools.partial(kernel, n, nk, norb),
        out_shape=jax.ShapeDtypeStruct((size, columns), bf16),
        in_specs=[vmem, vmem, pl.BlockSpec(memory_space=pl.ANY), vmem, vmem],
        out_specs=vmem,
        scratch_shapes=[
            pltpu.VMEM((n, 1, nchol), f32),
            pltpu.VMEM((128, 128 * ROWS), bf16),
            pltpu.VMEM((n * ROWS, nchol * ROWS), bf16),
            pltpu.VMEM((SLOTS, nchol, ROWS, cols), bf16),
            pltpu.VMEM((n * ROWS, cols), f32),
            pltpu.VMEM((chunks, n, ROWS, cols), bf16),
            pltpu.VMEM((chunks, n, ROWS, cols), bf16),
            pltpu.VMEM((size, size), bf16),
            pltpu.VMEM((size, 128), f32),
            pltpu.VMEM((size, columns), f32),
            pltpu.VMEM((size, columns), bf16),
            pltpu.VMEM((size, columns), bf16),
            pltpu.SemaphoreType.DMA((n,)),
            pltpu.SemaphoreType.DMA((n,)),
            pltpu.SemaphoreType.DMA((SLOTS,)),
            pltpu.SemaphoreType.DMA((chunks, n)),
            pltpu.SemaphoreType.DMA((chunks, n)),
        ],
        compiler_params=pltpu.CompilerParams(
            collective_id=0, has_side_effects=True, vmem_limit_bytes=60 * 1024 * 1024
        ),
    )(
        fields.reshape(nk, 1, nchol), field_shift, cholesky, onebody,
        walkers.reshape(size, columns),
    )
    return out.reshape(walkers.shape)


def per_device(fields, field_shift, cholesky, onebody, walkers):
    n = lax.axis_size("pb")
    nk, norb = onebody.shape
    fits = (
        fields.shape[0] == 1 and n == nk and cholesky.shape[1] == norb and norb == 64
        and walkers.shape[2] % 128 == 0 and cholesky.shape[0] % 128 == 0
    )
    body = fused if fits else plain
    return body(fields, field_shift, cholesky, onebody, walkers)


def solution(mesh):
    return jax.shard_map(
        per_device,
        mesh=mesh,
        in_specs=(
            P(("groups", "pb"), None, None),
            P(),
            P(None, "pb", None),
            P(),
            P(("groups", "pb"), None, None),
        ),
        out_specs=P(("groups", "pb"), None, None),
        check_vma=False,
    )
```

```python
import functools

import jax
import jax.numpy as jnp
import numpy as np
from jax import lax
from jax.experimental import pallas as pl
from jax.experimental.pallas import tpu as pltpu
from jax.sharding import PartitionSpec as P

TERMS = 6
MESH = pl.DeviceIdType.MESH
ROWS = 16
SLOTS = 3
SPLITS = 2
PIECE = 2048


def plain(fields, field_shift, cholesky, onebody, walkers):
    devices = lax.axis_size("pb")
    local_walkers = fields.shape[0]
    kpoints = field_shift.shape[0]
    orbitals = onebody.shape[1]
    vectors = field_shift.shape[1]
    rows_here = cholesky.shape[1]
    per_transfer = orbitals // rows_here
    slab = cholesky.reshape(vectors, rows_here * kpoints * orbitals)
    shifted = (fields + field_shift[None]).astype(jnp.bfloat16)
    outgoing = jnp.repeat(shifted, per_transfer, axis=1)
    arrived = lax.all_to_all(outgoing, "pb", split_axis=1, concat_axis=0, tiled=True)
    partial_blocks = jnp.dot(arrived[:, 0, :], slab, preferred_element_type=jnp.float32).astype(
        jnp.bfloat16
    )
    outgoing_blocks = partial_blocks.reshape(devices, local_walkers, rows_here * kpoints * orbitals)
    relayed = lax.all_to_all(outgoing_blocks, "pb", split_axis=0, concat_axis=0, tiled=True)
    relayed = relayed.reshape(kpoints, per_transfer, local_walkers, rows_here, kpoints, orbitals)
    potential = relayed.transpose(2, 4, 1, 3, 0, 5).reshape(
        local_walkers, kpoints, orbitals, kpoints, orbitals
    )
    source_table = (np.arange(kpoints)[:, None] - np.arange(kpoints)[None, :]) % kpoints
    source_index = jnp.asarray(source_table.reshape(1, kpoints, 1, kpoints, 1), dtype=jnp.int32)
    permuted = jnp.take_along_axis(potential, source_index, axis=3)
    permuted = permuted.reshape(local_walkers, kpoints * orbitals, kpoints * orbitals)
    diagonal_term = onebody.reshape(kpoints * orbitals)[None, :, None]
    term = walkers
    total = term.astype(jnp.float32)
    for order in range(1, TERMS):
        product = jnp.einsum("wij,wjc->wic", permuted, term, preferred_element_type=jnp.float32)
        product = product + diagonal_term * term.astype(jnp.float32)
        term = (product * (-1.0 / order)).astype(jnp.bfloat16)
        total = total + term.astype(jnp.float32)
    return total.astype(jnp.bfloat16)


def kernel(
    n, nk, norb, fields_ref, shift_ref, onebody_ref, chol_ref, walker_hbm, out_ref,
    fields_out, fields_in, lines, spread, left, buf, acc, blocks_out, blocks_in, matrix, rows_in, diag,
    total, walker, term_a, term_b, fsend, frecv, csem, bsend, brecv, wsem,
):
    me = lax.axis_index("pb")
    nchol = chol_ref.shape[0]
    cols = chol_ref.shape[2] // SPLITS
    row_blocks = norb // ROWS
    chunks = row_blocks * SPLITS
    k_here = cols // norb
    group = 128
    wide = group * ROWS
    half = n // 2
    mine = me // half
    places = [r for r in range(n) if r != half]

    def peer_of(r):
        side = 1 - mine if r < half else mine
        return side * half + lax.rem(me + r % half, half)

    def tensor_copy(c, slot):
        i, h = c // SPLITS, c % SPLITS
        return pltpu.make_async_copy(
            chol_ref.at[:, pl.ds(pl.multiple_of(i * ROWS, ROWS), ROWS), pl.ds(pl.multiple_of(h * cols, cols), cols)],
            buf.at[slot],
            csem.at[slot],
        )

    barrier = pltpu.get_barrier_semaphore()
    for r in places:
        pl.semaphore_signal(barrier, inc=1, device_id={"pb": peer_of(r)}, device_id_type=MESH)
    for c in range(min(SLOTS, chunks)):
        tensor_copy(c, c).start()
    walker_copy = pltpu.make_async_copy(walker_hbm, walker, wsem)
    walker_copy.start()
    for q in range(nk):
        fields_out[q] = fields_ref[q : q + 1, :]
    fields_in[me] = fields_out[me]
    pl.semaphore_wait(barrier, n - 1)

    def field_copy(peer, slot, r):
        return pltpu.make_async_remote_copy(
            src_ref=fields_out.at[peer], dst_ref=fields_in.at[slot], send_sem=fsend.at[r],
            recv_sem=frecv.at[slot], device_id={"pb": peer}, device_id_type=MESH,
        )

    for r in places:
        field_copy(peer_of(r), me, r).start()

    spread[...] = (
        lax.broadcasted_iota(jnp.int32, (group, wide), 1) // ROWS
        == lax.broadcasted_iota(jnp.int32, (group, wide), 0)
    ).astype(jnp.float32).astype(jnp.bfloat16)
    square = lax.broadcasted_iota(jnp.int32, (norb, norb), 0) == lax.broadcasted_iota(
        jnp.int32, (norb, norb), 1
    )
    for k in range(nk):
        row = jnp.broadcast_to(onebody_ref[k : k + 1, :], (norb, norb))
        column = jnp.sum(jnp.where(square, row, 0.0), axis=1, keepdims=True)
        diag[k * norb : (k + 1) * norb, :] = jnp.broadcast_to(column, (norb, 128))

    for r in places:
        peer = peer_of(r)
        field_copy(peer, peer, r).wait_recv()
    for r in range(n):
        lines[r : r + 1, :] = fields_in[peer_of(r)]

    mask = (
        lax.broadcasted_iota(jnp.int32, (ROWS, wide), 1) % ROWS
        == lax.broadcasted_iota(jnp.int32, (ROWS, wide), 0)
    )
    band = half * ROWS

    def block_copy(c, peer, slot, r):
        return pltpu.make_async_remote_copy(
            src_ref=blocks_out.at[c, r], dst_ref=blocks_in.at[c, slot], send_sem=bsend.at[c, r],
            recv_sem=brecv.at[c, slot], device_id={"pb": peer}, device_id_type=MESH,
        )

    vectors_piece = PIECE // ROWS

    def build(part):
        shifted = (lines[...] + shift_ref[pl.ds(me, 1), :]).astype(jnp.bfloat16)
        for b in range(nchol // group):
            spreaded = jnp.dot(
                shifted[:, b * group : (b + 1) * group], spread[...],
                preferred_element_type=jnp.float32,
            )
            for r in range(part * half, (part + 1) * half):
                line = jnp.broadcast_to(spreaded[r : r + 1, :], (ROWS, wide))
                left[r * ROWS : (r + 1) * ROWS, b * wide : (b + 1) * wide] = jnp.where(
                    mask, line, 0.0
                ).astype(jnp.bfloat16)

    def multiply(c, part):
        slot = lax.rem(c, SLOTS)

        def piece(p, carry):
            right = buf[slot, pl.ds(p * vectors_piece, vectors_piece)].reshape(PIECE, cols)
            product = jnp.dot(
                left[pl.ds(pl.multiple_of(part * band, band), band), pl.ds(pl.multiple_of(p * PIECE, PIECE), PIECE)],
                right, preferred_element_type=jnp.float32,
            )

            @pl.when(p == 0)
            def _():
                acc[...] = product

            @pl.when(p > 0)
            def _():
                acc[...] += product

            return carry

        lax.fori_loop(0, nchol // vectors_piece, piece, 0)
        blocks_out[c, pl.ds(part * half, half)] = acc[...].astype(jnp.bfloat16).reshape(half, ROWS, cols)

    def compute(c, carry):
        slot = lax.rem(c, SLOTS)

        @pl.when(c == 0)
        def _():
            build(0)

        tensor_copy(c, slot).wait()
        for part in range(2):
            if part == 1:

                @pl.when(c == 0)
                def _():
                    build(1)

            multiply(c, part)
            for r in places:
                if r // half == part:
                    block_copy(c, peer_of(r), me, r).start()
        blocks_in[c, me] = blocks_out[c, half]

        @pl.when(c + SLOTS < chunks)
        def _():
            tensor_copy(c + SLOTS, slot).start()

        return carry

    lax.fori_loop(0, chunks, compute, 0)
    walker_copy.wait()

    def finish(product, here, weight, number):
        weight = jnp.concatenate([weight] * (here.shape[1] // 128), axis=1)
        return ((product + weight * here) * (-1.0 / number)).astype(jnp.bfloat16)

    def assemble(c, carry):
        i, h = c // SPLITS, c % SPLITS
        for r in places:
            peer = peer_of(r)
            block_copy(c, peer, peer, r).wait_recv()
        for kk in range(k_here):
            k = h * k_here + kk
            lane = kk // 2 * 128
            off = kk % 2 * norb
            rows = pl.ds(pl.multiple_of(k * norb + i * ROWS, ROWS), ROWS)
            for pair in range(nk // 2):
                first = blocks_in[c, lax.rem(k - 2 * pair + nk, nk), :, lane : lane + 128]
                second = blocks_in[c, lax.rem(k - 2 * pair - 1 + nk, nk), :, lane : lane + 128]
                both = jnp.concatenate([first[:, off : off + norb], second[:, off : off + norb]], axis=1)
                matrix[rows, pair * 128 : (pair + 1) * 128] = both
                rows_in[kk * ROWS : (kk + 1) * ROWS, pair * 128 : (pair + 1) * 128] = both
        product = jnp.dot(rows_in[...], walker[...], preferred_element_type=jnp.float32)
        for kk in range(k_here):
            rows = pl.ds(pl.multiple_of((h * k_here + kk) * norb + i * ROWS, ROWS), ROWS)
            here = walker[rows, :].astype(jnp.float32)
            term = finish(product[kk * ROWS : (kk + 1) * ROWS], here, diag[rows, :], 1)
            term_a[rows, :] = term
            total[rows, :] = here + term.astype(jnp.float32)
        return carry

    lax.fori_loop(0, chunks, assemble, 0)

    size = nk * norb
    step = 256
    for number in range(2, TERMS):
        source, target = (term_a, term_b) if number % 2 == 0 else (term_b, term_a)
        for r in range(0, size, step):
            rows = slice(r, r + step)
            product = jnp.dot(matrix[rows, :], source[...], preferred_element_type=jnp.float32)
            term = finish(product, source[rows, :].astype(jnp.float32), diag[rows, :], number)
            after = total[rows, :] + term.astype(jnp.float32)
            if number < TERMS - 1:
                target[rows, :] = term
                total[rows, :] = after
            else:
                out_ref[rows, :] = after.astype(jnp.bfloat16)

    for r in places:
        field_copy(peer_of(r), me, r).wait_send()

    def drain(c, carry):
        for r in places:
            block_copy(c, peer_of(r), me, r).wait_send()
        return carry

    lax.fori_loop(0, chunks, drain, 0)


def fused(fields, field_shift, cholesky, onebody, walkers):
    n = lax.axis_size("pb")
    nk, norb = onebody.shape
    nchol = cholesky.shape[0]
    width = cholesky.shape[2]
    cols = width // SPLITS
    chunks = norb // ROWS * SPLITS
    size, columns = walkers.shape[1:]
    bf16, f32 = jnp.bfloat16, jnp.float32
    vmem = pl.BlockSpec(memory_space=pltpu.VMEM)
    hbm = pl.BlockSpec(memory_space=pl.ANY)
    out = pl.pallas_call(
        functools.partial(kernel, n, nk, norb),
        out_shape=jax.ShapeDtypeStruct((size, columns), bf16),
        in_specs=[vmem, vmem, vmem, hbm, hbm],
        out_specs=vmem,
        scratch_shapes=[
            pltpu.VMEM((nk, 1, nchol), f32),
            pltpu.VMEM((n, 1, nchol), f32),
            pltpu.VMEM((n, nchol), f32),
            pltpu.VMEM((128, 128 * ROWS), bf16),
            pltpu.VMEM((n * ROWS, nchol * ROWS), bf16),
            pltpu.VMEM((SLOTS, nchol, ROWS, cols), bf16),
            pltpu.VMEM((n // 2 * ROWS, cols), f32),
            pltpu.VMEM((chunks, n, ROWS, cols), bf16),
            pltpu.VMEM((chunks, n, ROWS, cols), bf16),
            pltpu.VMEM((size, size), bf16),
            pltpu.VMEM((cols // norb * ROWS, size), bf16),
            pltpu.VMEM((size, 128), f32),
            pltpu.VMEM((size, columns), f32),
            pltpu.VMEM((size, columns), bf16),
            pltpu.VMEM((size, columns), bf16),
            pltpu.VMEM((size, columns), bf16),
            pltpu.SemaphoreType.DMA((n,)),
            pltpu.SemaphoreType.DMA((n,)),
            pltpu.SemaphoreType.DMA((SLOTS,)),
            pltpu.SemaphoreType.DMA((chunks, n)),
            pltpu.SemaphoreType.DMA((chunks, n)),
            pltpu.SemaphoreType.DMA,
        ],
        compiler_params=pltpu.CompilerParams(
            collective_id=0, has_side_effects=True, vmem_limit_bytes=60 * 1024 * 1024
        ),
    )(
        fields.reshape(nk, nchol), field_shift, onebody, cholesky,
        walkers.reshape(size, columns),
    )
    return out.reshape(walkers.shape)


def per_device(fields, field_shift, cholesky, onebody, walkers):
    n = lax.axis_size("pb")
    nk, norb = onebody.shape
    fits = (
        fields.shape[0] == 1 and n == nk and cholesky.shape[1] == norb and norb == 64
        and walkers.shape[2] % 128 == 0 and cholesky.shape[0] % 128 == 0
    )
    body = fused if fits else plain
    return body(fields, field_shift, cholesky, onebody, walkers)


def solution(mesh):
    return jax.shard_map(
        per_device,
        mesh=mesh,
        in_specs=(
            P(("groups", "pb"), None, None),
            P(),
            P(None, "pb", None),
            P(),
            P(("groups", "pb"), None, None),
        ),
        out_specs=P(("groups", "pb"), None, None),
        check_vma=False,
    )
```

```python
import functools

import jax
import jax.numpy as jnp
import numpy as np
from jax import lax
from jax.experimental import pallas as pl
from jax.experimental.pallas import tpu as pltpu
from jax.sharding import PartitionSpec as P

TERMS = 6
MESH = pl.DeviceIdType.MESH
ROWS = 16
SLOTS = 3
SPLITS = 2
PIECE = 2048


def plain(fields, field_shift, cholesky, onebody, walkers):
    devices = lax.axis_size("pb")
    local_walkers = fields.shape[0]
    kpoints = field_shift.shape[0]
    orbitals = onebody.shape[1]
    vectors = field_shift.shape[1]
    rows_here = cholesky.shape[1]
    per_transfer = orbitals // rows_here
    slab = cholesky.reshape(vectors, rows_here * kpoints * orbitals)
    shifted = (fields + field_shift[None]).astype(jnp.bfloat16)
    outgoing = jnp.repeat(shifted, per_transfer, axis=1)
    arrived = lax.all_to_all(outgoing, "pb", split_axis=1, concat_axis=0, tiled=True)
    partial_blocks = jnp.dot(arrived[:, 0, :], slab, preferred_element_type=jnp.float32).astype(
        jnp.bfloat16
    )
    outgoing_blocks = partial_blocks.reshape(devices, local_walkers, rows_here * kpoints * orbitals)
    relayed = lax.all_to_all(outgoing_blocks, "pb", split_axis=0, concat_axis=0, tiled=True)
    relayed = relayed.reshape(kpoints, per_transfer, local_walkers, rows_here, kpoints, orbitals)
    potential = relayed.transpose(2, 4, 1, 3, 0, 5).reshape(
        local_walkers, kpoints, orbitals, kpoints, orbitals
    )
    source_table = (np.arange(kpoints)[:, None] - np.arange(kpoints)[None, :]) % kpoints
    source_index = jnp.asarray(source_table.reshape(1, kpoints, 1, kpoints, 1), dtype=jnp.int32)
    permuted = jnp.take_along_axis(potential, source_index, axis=3)
    permuted = permuted.reshape(local_walkers, kpoints * orbitals, kpoints * orbitals)
    diagonal_term = onebody.reshape(kpoints * orbitals)[None, :, None]
    term = walkers
    total = term.astype(jnp.float32)
    for order in range(1, TERMS):
        product = jnp.einsum("wij,wjc->wic", permuted, term, preferred_element_type=jnp.float32)
        product = product + diagonal_term * term.astype(jnp.float32)
        term = (product * (-1.0 / order)).astype(jnp.bfloat16)
        total = total + term.astype(jnp.float32)
    return total.astype(jnp.bfloat16)


def kernel(
    n, nk, norb, fields_ref, shift_ref, onebody_ref, chol_ref, walker_hbm, out_ref,
    fields_out, fields_in, lines, spread, left, buf, acc, blocks_out, blocks_in, matrix, rows_in, diag,
    total, walker, term_a, term_b, fsend, frecv, csem, bsend, brecv, wsem,
):
    me = lax.axis_index("pb")
    nchol = chol_ref.shape[0]
    cols = chol_ref.shape[2] // SPLITS
    row_blocks = norb // ROWS
    chunks = row_blocks * SPLITS
    k_here = cols // norb
    group = 128
    wide = group * ROWS
    half = n // 2
    mine = me // half
    places = [r for r in range(n) if r != half]

    def peer_of(r):
        side = 1 - mine if r < half else mine
        return side * half + lax.rem(me + r % half, half)

    def tensor_copy(c, slot):
        i, h = c // SPLITS, c % SPLITS
        return pltpu.make_async_copy(
            chol_ref.at[:, pl.ds(pl.multiple_of(i * ROWS, ROWS), ROWS), pl.ds(pl.multiple_of(h * cols, cols), cols)],
            buf.at[slot],
            csem.at[slot],
        )

    barrier = pltpu.get_barrier_semaphore()
    for r in places:
        pl.semaphore_signal(barrier, inc=1, device_id={"pb": peer_of(r)}, device_id_type=MESH)
    for c in range(min(SLOTS, chunks)):
        tensor_copy(c, c).start()
    walker_copy = pltpu.make_async_copy(walker_hbm, walker, wsem)
    walker_copy.start()
    for q in range(nk):
        fields_out[q] = fields_ref[q : q + 1, :]
    fields_in[me] = fields_out[me]
    spread[...] = (
        lax.broadcasted_iota(jnp.int32, (group, wide), 1) // ROWS
        == lax.broadcasted_iota(jnp.int32, (group, wide), 0)
    ).astype(jnp.float32).astype(jnp.bfloat16)
    pl.semaphore_wait(barrier, n - 1)

    def field_copy(peer, slot, r):
        return pltpu.make_async_remote_copy(
            src_ref=fields_out.at[peer], dst_ref=fields_in.at[slot], send_sem=fsend,
            recv_sem=frecv, device_id={"pb": peer}, device_id_type=MESH,
        )

    for r in places:
        field_copy(peer_of(r), me, r).start()

    others = pl.ds(0, n - 1)
    all_fields = pltpu.make_async_remote_copy(
        src_ref=fields_out.at[others], dst_ref=fields_in.at[others], send_sem=fsend,
        recv_sem=frecv, device_id={"pb": peer_of(0)}, device_id_type=MESH,
    )
    all_fields.wait_recv()
    for r in range(n):
        lines[r : r + 1, :] = fields_in[peer_of(r)]

    mask = (
        lax.broadcasted_iota(jnp.int32, (ROWS, wide), 1) % ROWS
        == lax.broadcasted_iota(jnp.int32, (ROWS, wide), 0)
    )
    band = half * ROWS

    def block_copy(c, peer, slot, r):
        return pltpu.make_async_remote_copy(
            src_ref=blocks_out.at[c, r], dst_ref=blocks_in.at[c, slot], send_sem=bsend,
            recv_sem=brecv.at[c], device_id={"pb": peer}, device_id_type=MESH,
        )

    vectors_piece = PIECE // ROWS

    def build(part):
        shifted = (lines[...] + shift_ref[pl.ds(me, 1), :]).astype(jnp.bfloat16)
        for b in range(nchol // group):
            spreaded = jnp.dot(
                shifted[:, b * group : (b + 1) * group], spread[...],
                preferred_element_type=jnp.float32,
            )
            for r in range(part * half, (part + 1) * half):
                line = jnp.broadcast_to(spreaded[r : r + 1, :], (ROWS, wide))
                left[r * ROWS : (r + 1) * ROWS, b * wide : (b + 1) * wide] = jnp.where(
                    mask, line, 0.0
                ).astype(jnp.bfloat16)

    def multiply(c, part):
        slot = lax.rem(c, SLOTS)

        def piece(p, carry):
            right = buf[slot, pl.ds(p * vectors_piece, vectors_piece)].reshape(PIECE, cols)
            product = jnp.dot(
                left[pl.ds(pl.multiple_of(part * band, band), band), pl.ds(pl.multiple_of(p * PIECE, PIECE), PIECE)],
                right, preferred_element_type=jnp.float32,
            )

            @pl.when(p == 0)
            def _():
                acc[...] = product

            @pl.when(p > 0)
            def _():
                acc[...] += product

            return carry

        lax.fori_loop(0, nchol // vectors_piece, piece, 0)
        blocks_out[c, pl.ds(part * half, half)] = acc[...].astype(jnp.bfloat16).reshape(half, ROWS, cols)

    def compute(c, carry):
        slot = lax.rem(c, SLOTS)

        @pl.when(c == 0)
        def _():
            build(0)

        tensor_copy(c, slot).wait()
        for part in range(2):
            if part == 1:

                @pl.when(c == 0)
                def _():
                    build(1)

            multiply(c, part)
            for r in places:
                if r // half == part:
                    block_copy(c, peer_of(r), me, r).start()
        blocks_in[c, me] = blocks_out[c, half]

        @pl.when(c + SLOTS < chunks)
        def _():
            tensor_copy(c + SLOTS, slot).start()

        return carry

    lax.fori_loop(0, chunks, compute, 0)
    square = lax.broadcasted_iota(jnp.int32, (norb, norb), 0) == lax.broadcasted_iota(
        jnp.int32, (norb, norb), 1
    )
    for k in range(nk):
        row = jnp.broadcast_to(onebody_ref[k : k + 1, :], (norb, norb))
        column = jnp.sum(jnp.where(square, row, 0.0), axis=1, keepdims=True)
        diag[k * norb : (k + 1) * norb, :] = jnp.broadcast_to(column, (norb, 128))

    walker_copy.wait()

    def finish(product, here, weight, number):
        weight = jnp.concatenate([weight] * (here.shape[1] // 128), axis=1)
        return ((product + weight * here) * (-1.0 / number)).astype(jnp.bfloat16)

    def assemble(c, carry):
        i, h = c // SPLITS, c % SPLITS
        pltpu.make_async_remote_copy(
            src_ref=blocks_out.at[c, others], dst_ref=blocks_in.at[c, others], send_sem=bsend,
            recv_sem=brecv.at[c], device_id={"pb": peer_of(0)}, device_id_type=MESH,
        ).wait_recv()
        for kk in range(k_here):
            k = h * k_here + kk
            lane = kk // 2 * 128
            off = kk % 2 * norb
            rows = pl.ds(pl.multiple_of(k * norb + i * ROWS, ROWS), ROWS)
            for pair in range(nk // 2):
                first = blocks_in[c, lax.rem(k - 2 * pair + nk, nk), :, lane : lane + 128]
                second = blocks_in[c, lax.rem(k - 2 * pair - 1 + nk, nk), :, lane : lane + 128]
                both = jnp.concatenate([first[:, off : off + norb], second[:, off : off + norb]], axis=1)
                matrix[rows, pair * 128 : (pair + 1) * 128] = both
                rows_in[kk * ROWS : (kk + 1) * ROWS, pair * 128 : (pair + 1) * 128] = both
        product = jnp.dot(rows_in[...], walker[...], preferred_element_type=jnp.float32)
        for kk in range(k_here):
            rows = pl.ds(pl.multiple_of((h * k_here + kk) * norb + i * ROWS, ROWS), ROWS)
            here = walker[rows, :].astype(jnp.float32)
            term = finish(product[kk * ROWS : (kk + 1) * ROWS], here, diag[rows, :], 1)
            term_a[rows, :] = term
            total[rows, :] = here + term.astype(jnp.float32)
        return carry

    lax.fori_loop(0, chunks, assemble, 0)

    size = nk * norb
    step = 256
    for number in range(2, TERMS):
        source, target = (term_a, term_b) if number % 2 == 0 else (term_b, term_a)
        for r in range(0, size, step):
            rows = slice(r, r + step)
            product = jnp.dot(matrix[rows, :], source[...], preferred_element_type=jnp.float32)
            term = finish(product, source[rows, :].astype(jnp.float32), diag[rows, :], number)
            after = total[rows, :] + term.astype(jnp.float32)
            if number < TERMS - 1:
                target[rows, :] = term
                total[rows, :] = after
            else:
                out_ref[rows, :] = after.astype(jnp.bfloat16)

    all_fields.wait_send()
    pltpu.make_async_remote_copy(
        src_ref=blocks_out.at[:, others], dst_ref=blocks_in.at[:, others], send_sem=bsend,
        recv_sem=brecv.at[0], device_id={"pb": peer_of(0)}, device_id_type=MESH,
    ).wait_send()


def fused(fields, field_shift, cholesky, onebody, walkers):
    n = lax.axis_size("pb")
    nk, norb = onebody.shape
    nchol = cholesky.shape[0]
    width = cholesky.shape[2]
    cols = width // SPLITS
    chunks = norb // ROWS * SPLITS
    size, columns = walkers.shape[1:]
    bf16, f32 = jnp.bfloat16, jnp.float32
    vmem = pl.BlockSpec(memory_space=pltpu.VMEM)
    hbm = pl.BlockSpec(memory_space=pl.ANY)
    out = pl.pallas_call(
        functools.partial(kernel, n, nk, norb),
        out_shape=jax.ShapeDtypeStruct((size, columns), bf16),
        in_specs=[vmem, vmem, vmem, hbm, hbm],
        out_specs=vmem,
        scratch_shapes=[
            pltpu.VMEM((nk, 1, nchol), f32),
            pltpu.VMEM((n, 1, nchol), f32),
            pltpu.VMEM((n, nchol), f32),
            pltpu.VMEM((128, 128 * ROWS), bf16),
            pltpu.VMEM((n * ROWS, nchol * ROWS), bf16),
            pltpu.VMEM((SLOTS, nchol, ROWS, cols), bf16),
            pltpu.VMEM((n // 2 * ROWS, cols), f32),
            pltpu.VMEM((chunks, n, ROWS, cols), bf16),
            pltpu.VMEM((chunks, n, ROWS, cols), bf16),
            pltpu.VMEM((size, size), bf16),
            pltpu.VMEM((cols // norb * ROWS, size), bf16),
            pltpu.VMEM((size, 128), f32),
            pltpu.VMEM((size, columns), f32),
            pltpu.VMEM((size, columns), bf16),
            pltpu.VMEM((size, columns), bf16),
            pltpu.VMEM((size, columns), bf16),
            pltpu.SemaphoreType.DMA,
            pltpu.SemaphoreType.DMA,
            pltpu.SemaphoreType.DMA((SLOTS,)),
            pltpu.SemaphoreType.DMA,
            pltpu.SemaphoreType.DMA((chunks,)),
            pltpu.SemaphoreType.DMA,
        ],
        compiler_params=pltpu.CompilerParams(
            collective_id=0, has_side_effects=True, vmem_limit_bytes=60 * 1024 * 1024
        ),
    )(
        fields.reshape(nk, nchol), field_shift, onebody, cholesky,
        walkers.reshape(size, columns),
    )
    return out.reshape(walkers.shape)


def per_device(fields, field_shift, cholesky, onebody, walkers):
    n = lax.axis_size("pb")
    nk, norb = onebody.shape
    fits = (
        fields.shape[0] == 1 and n == nk and cholesky.shape[1] == norb and norb == 64
        and walkers.shape[2] % 128 == 0 and cholesky.shape[0] % 128 == 0
    )
    body = fused if fits else plain
    return body(fields, field_shift, cholesky, onebody, walkers)


def solution(mesh):
    return jax.shard_map(
        per_device,
        mesh=mesh,
        in_specs=(
            P(("groups", "pb"), None, None),
            P(),
            P(None, "pb", None),
            P(),
            P(("groups", "pb"), None, None),
        ),
        out_specs=P(("groups", "pb"), None, None),
        check_vma=False,
    )
```
